32 devices in a mesh: batch: 8 (over z, y), tensor: 4 (over x, core).
Axes of the slice: x: 2, y: 2, z: 4, core: 2. Of those that a mesh axis runs over, the one named last changes fastest.
Arguments:
- target_latents: bfloat16 [2048, 2048], P('batch', 'tensor'), may hold values from -6 to 6
- walk_noise: bfloat16 [4, 2048, 2048], P(None, 'batch', 'tensor'), may hold values from -6 to 6
- step_sizes: float32 [4], replicated, may hold values from 0.05 to 0.2
- back_gain: float32 [2048], replicated, may hold values from 0.1 to 1.9
- back_expand: bfloat16 [2048, 4096], P(None, 'tensor'), may hold values from -0.125 to 0.125
- back_clock: float32 [4096], P('tensor'), may hold values from -4 to 4
- back_reduce: bfloat16 [4096, 2048], P('tensor'), may hold values from -0.09375 to 0.09375
- bridge_times: float32 [2048], P('batch'), may hold values from 0.05 to 0.9
- bridge_noise: bfloat16 [2048, 2048], P('batch', 'tensor'), may hold values from -6 to 6
- fore_gain: float32 [2048], replicated, may hold values from 0.1 to 1.9
- fore_expand: bfloat16 [2048, 4096], P(None, 'tensor'), may hold values from -0.125 to 0.125
- fore_clock: float32 [4096], P('tensor'), may hold values from -4 to 4
- fore_reduce: bfloat16 [4096, 2048], P('tensor'), may hold values from -0.09375 to 0.09375
Outputs:
- walk_end: float32 [2048, 2048], P('batch', 'tensor')
- grad_expand: float32 [2048, 4096], P('batch', 'tensor')
- grad_reduce_t: float32 [2048, 4096], P('batch', 'tensor')
The draws below stay inside these ranges and needn't reach their ends.
All inputs are finite; a program needn't handle non-finite values.
Results may differ from the reference program's by a relative error of at most 0.0055.
Values may be sent and summed in bfloat16 or wider, within the bound.
No kernel may reach another device: no remote copies, remote signals or barrier semaphores. Data moves between devices by JAX's collectives and lax.ppermute only.
A program may use at most 128 MiB of HBM per device.

```python
import math
import jax
import jax.numpy as jnp
from jax import lax

D = 2048
FF = 4096
STEPS = 4
TOK_DEV = 256
TOKENS = 2048
N_BATCH = 8


def raised(values, stream_key, source, target, parts, factor):
    owner, partner = [(jnp.arange(values.shape[axis_at]) // (values.shape[axis_at] // parts)).reshape([-1 if axis == axis_at else 1 for axis in range(values.ndim)]) for axis_at in (source, target)]
    chosen = jax.random.permutation(stream_key, parts)[partner]
    strong = (owner == chosen) | (owner == (partner + parts // 2) % parts)
    return jnp.where(strong, factor * values, values)


def shard_levels(stream_key, extent, split, smallest, largest):
    factor_of, own = 1.0, jax.random.fold_in(stream_key, 6)
    for dim, parts in split:
        steps = jnp.exp(jax.random.uniform(jax.random.fold_in(own, dim), (parts,), jnp.float32, smallest / len(split), largest / len(split)))
        factor_of = factor_of * jnp.repeat(steps, extent[dim] // parts).reshape([-1 if axis == dim else 1 for axis in range(len(extent))])
    return factor_of


def centred(key, dims, spread, most, cuts=(), kind=jnp.bfloat16):
    level = shard_levels(key, dims, cuts, -0.22, 0.18) if cuts else 1.0
    result = jax.random.normal(key, dims, jnp.float32) * spread * level
    return jnp.minimum(jnp.maximum(result, -most), most).astype(kind)


def noise_with(key, shape, scale, reach, split, heavy, dtype=jnp.bfloat16):
    values = scale * jax.random.normal(key, shape, jnp.float32)
    if split:
        values = values * shard_levels(key, shape, split, -0.22, 0.18)
    return jnp.clip(raised(values, jax.random.fold_in(key, 3), *heavy), -reach, reach).astype(dtype)


def setup_inputs(seed: int = 0) -> dict:
    keys = jax.random.split(jax.random.key(seed), 14)
    target_latents = centred(keys[0], (TOKENS, D), 1.0, 6.0, ((0, 8), (1, 4)))
    walk_noise = centred(keys[1], (STEPS, TOKENS, D), 1.0, 6.0, ((1, 8), (2, 4)))
    step_sizes = jnp.clip(jnp.exp(jax.random.uniform(keys[2], (STEPS,), jnp.float32, math.log(0.05), math.log(0.2))), 0.05, 0.2)
    back_gain = jnp.clip(1.0 + 0.18 * jax.random.normal(keys[3], (D,), jnp.float32), 0.1, 1.9)
    back_expand = centred(keys[4], (D, FF), D ** -0.5, 0.125, ((1, 4),))
    back_clock = centred(keys[5], (FF,), 1.0, 4.0, ((0, 4),), jnp.float32)
    back_reduce = centred(keys[6], (FF, D), FF ** -0.5, 0.09375, ((0, 4),))
    bridge_times = jnp.clip(0.05 + 0.84999998 * jax.random.uniform(keys[7], (TOKENS,), jnp.float32) ** shard_levels(keys[7], (TOKENS,), ((0, 8),), -0.2, 0.2), 0.05, 0.9)
    bridge_noise = noise_with(keys[8], (TOKENS, D), 1.0, 6.0, ((0, 8), (1, 4)), (0, 1, 8, 2.0))
    fore_gain = jnp.clip(1.0 + 0.18 * jax.random.normal(keys[9], (D,), jnp.float32), 0.1, 1.9)
    fore_expand = centred(keys[10], (D, FF), D ** -0.5, 0.125, ((1, 4),))
    fore_clock = centred(keys[11], (FF,), 1.0, 4.0, ((0, 4),), jnp.float32)
    fore_reduce = centred(keys[12], (FF, D), FF ** -0.5, 0.09375, ((0, 4),))
    return dict(target_latents=target_latents, walk_noise=walk_noise, step_sizes=step_sizes, back_gain=back_gain, back_expand=back_expand, back_clock=back_clock, back_reduce=back_reduce, bridge_times=bridge_times, bridge_noise=bridge_noise, fore_gain=fore_gain, fore_expand=fore_expand, fore_clock=fore_clock, fore_reduce=fore_reduce)


NOISE_LEVEL = 0.5
EPSILON = 1e-06

def normalize(rows, gain):
    float_rows = rows.astype(jnp.float32)
    factor = lax.rsqrt(lax.optimization_barrier(jnp.mean(float_rows * float_rows, axis=1, keepdims=True)) + EPSILON)
    return (float_rows * factor * gain).astype(jnp.bfloat16)

def regroup(array):
    pieces = array.reshape(N_BATCH, N_BATCH, TOK_DEV // N_BATCH, D)
    return jnp.swapaxes(pieces, 0, 1).reshape(TOKENS, D)

def reference(target_latents, walk_noise, step_sizes, back_gain, back_expand, back_clock, back_reduce, bridge_times, bridge_noise, fore_gain, fore_expand, fore_clock, fore_reduce):
    walk_state = target_latents.astype(jnp.float32)
    walk_clock = jnp.float32(1.0)
    for step_index in range(STEPS):
        normed = normalize(walk_state.astype(jnp.bfloat16), back_gain)
        hidden = jnp.dot(normed, back_expand, preferred_element_type=jnp.float32) + walk_clock * back_clock
        active = jax.nn.silu(hidden).astype(jnp.bfloat16)
        drift = jnp.dot(active, back_reduce, preferred_element_type=jnp.float32)
        step_width = step_sizes[step_index]
        walk_state = walk_state - step_width * drift + jnp.sqrt(step_width) * NOISE_LEVEL * walk_noise[step_index].astype(jnp.float32)
        walk_clock = walk_clock - step_width
    walk_end = walk_state
    start_float = regroup(walk_end.astype(jnp.bfloat16)).astype(jnp.float32)
    end_float = regroup(target_latents).astype(jnp.float32)
    bridge_tau = bridge_times[:, None]
    interpolant = (1.0 - bridge_tau) * start_float + bridge_tau * end_float + jnp.sqrt(bridge_tau * (1.0 - bridge_tau)) * NOISE_LEVEL * bridge_noise.astype(jnp.float32)
    target_flow = (end_float - interpolant) / (1.0 - bridge_tau)
    normed = normalize(interpolant.astype(jnp.bfloat16), fore_gain)
    hidden = jnp.dot(normed, fore_expand, preferred_element_type=jnp.float32) + bridge_tau * fore_clock
    active = jax.nn.silu(hidden).astype(jnp.bfloat16)
    predicted = jnp.dot(active, fore_reduce, preferred_element_type=jnp.float32)
    loss_scale = 1.0 / jnp.sqrt(jnp.float32(TOKENS))
    scaled_error = ((predicted - target_flow) * loss_scale).astype(jnp.bfloat16)
    back_hidden = lax.dot_general(scaled_error, fore_reduce, (((1,), (1,)), ((), ())), preferred_element_type=jnp.float32)
    sigmoid_part = jax.nn.sigmoid(hidden)
    silu_slope = sigmoid_part * (1.0 + hidden * (1.0 - sigmoid_part))
    hidden_grad = (back_hidden * silu_slope).astype(jnp.bfloat16)
    grad_expand = lax.dot_general(normed, hidden_grad, (((0,), (0,)), ((), ())), preferred_element_type=jnp.float32)
    grad_reduce_t = lax.dot_general(scaled_error, active, (((0,), (0,)), ((), ())), preferred_element_type=jnp.float32)
    return (walk_end, grad_expand, grad_reduce_t)
```

```python
import functools

import jax
import jax.numpy as jnp
from jax import lax
from jax.experimental import pallas as pl
from jax.experimental.pallas import tpu as pltpu
from jax.sharding import PartitionSpec as P

NOISE_LEVEL = 0.5
EPSILON = 1e-06
CHUNKS = 2
TILE = 256

bf16 = jnp.bfloat16
f32 = jnp.float32
VMEM = pl.BlockSpec(memory_space=pltpu.VMEM)
SMEM = pl.BlockSpec(memory_space=pltpu.SMEM)
ANY = pl.BlockSpec(memory_space=pl.ANY)


def call(kernel, outs, ins, args, scratch=(), flops=0, limit=24):
    moved = sum(a.size * a.dtype.itemsize for a in args)
    moved += sum(o.size * o.dtype.itemsize for o in outs)
    return pl.pallas_call(
        kernel,
        out_shape=tuple(outs),
        in_specs=list(ins),
        out_specs=tuple(VMEM for _ in outs),
        scratch_shapes=list(scratch),
        compiler_params=pltpu.CompilerParams(vmem_limit_bytes=limit << 20),
        cost_estimate=pl.CostEstimate(flops=flops, bytes_accessed=moved, transcendentals=0),
    )(*args)


def shape(dims, dtype):
    return jax.ShapeDtypeStruct(dims, dtype)


def dot(a, b):
    return jnp.dot(a, b, preferred_element_type=f32)


def block_of(core, x, width):
    return pl.multiple_of((2 * x + core) * width, width)


def core_of():
    return lax.rem(lax.axis_index("tensor"), 2)


def x_of():
    return lax.div(lax.axis_index("tensor"), 2)


def ring_place(index, size):
    level = lax.div(index, 2)
    return jnp.where(lax.rem(index, 2) == 0, level, size - 1 - level)


def ring_index(place, size):
    return jnp.where(place < size // 2, 2 * place, 2 * (size - 1 - place) + 1)


def before(shift, size):
    place = ring_place(lax.axis_index("batch"), size)
    return ring_index(lax.rem(place - shift + size, size), size)


def pack_kernel(noise, times, out):
    width = noise.shape[1]
    t = times[...]
    high = t.astype(bf16).astype(f32)
    middle = (t - high).astype(bf16).astype(f32)
    low = t - high - middle
    lane = lax.broadcasted_iota(jnp.int32, (t.shape[0], 128), 1)
    terms = jnp.where(lane == 0, high, jnp.where(lane == 1, middle, low))
    out[:, :width] = noise[...]
    out[:, width:] = jnp.where(lane < 3, terms, 0.0).astype(bf16)


def unpack_kernel(packed, noise, times):
    width = noise.shape[1]
    noise[...] = packed[:, :width]
    times[...] = jnp.sum(packed[:, width:].astype(f32), axis=1, keepdims=True)


def join_kernel(mine, *refs, width):
    *others, half, state = refs
    x = x_of()
    count = len(others) + 1
    half[:, pl.ds(pl.multiple_of(x * width, width), width)] = mine[...]
    for shift, other in enumerate(others):
        at = lax.rem(x + shift + 1, count)
        half[:, pl.ds(pl.multiple_of(at * width, width), width)] = other[...]
    state[...] = half[...].astype(f32)


def norm_into(normed, own, other, gain, width):
    core = core_of()
    a = own[...].astype(f32)
    b = other[...].astype(f32)
    features = gain.shape[1]
    square = jnp.sum(a * a, axis=1, keepdims=True) + jnp.sum(b * b, axis=1, keepdims=True)
    factor = lax.rsqrt(square / features + EPSILON)
    for who, rows in ((core, a), (1 - core, b)):
        for x in range(rows.shape[1] // width):
            at = block_of(who, x, width)
            part = rows[:, x * width : (x + 1) * width] * factor * gain[:, pl.ds(at, width)]
            normed[:, pl.ds(at, width)] = part.astype(bf16)


def reduce_out(active, reduce, other_out, own_out, width):
    core = core_of()
    for who, out in ((1 - core, other_out), (core, own_out)):
        for x in range(out.shape[1] // width):
            for tile in range(width // TILE):
                at = pl.multiple_of(block_of(who, x, width) + tile * TILE, TILE)
                product = dot(active[...], reduce[:, pl.ds(at, TILE)])
                start = x * width + tile * TILE
                out[:, start : start + TILE] = product.astype(out.dtype)


def walk_kernel(sizes, own, other, gain, expand, clock, reduce, other_out, own_out, normed, active, *, width, step):
    norm_into(normed, own, other, gain, width)
    time = 1.0
    for past in range(step):
        time = time - sizes[past]
    for start in range(0, expand.shape[1], TILE):
        cut = slice(start, start + TILE)
        hidden = dot(normed[...], expand[:, cut]) + time * clock[:, cut]
        active[:, cut] = (hidden / (1.0 + jnp.exp(-hidden))).astype(bf16)
    reduce_out(active, reduce, other_out, own_out, width)


def move_kernel(sizes, own, other, state, noise, sent, moved, *, width, step, rows):
    change = -sizes[step] * (own[...] + other[...].astype(f32))
    spread = jnp.sqrt(jnp.full((1, width), sizes[step], f32)) * NOISE_LEVEL
    moved[...] = change
    at = pl.ds(pl.multiple_of(x_of() * width, width), width)
    moved[:, at] += spread * noise[step, rows, :].astype(f32)
    sent[...] = moved[...].astype(bf16)
    moved[...] += state[...]


def land_kernel(moved, *refs, count):
    *others, state, short = refs[: count - 1] + refs[-2:]
    value = moved[...]
    for other in others:
        value = value + other[...].astype(f32)
    state[...] = value
    short[...] = value.astype(bf16)


def bridge_kernel(moved, end, times, noise_mine, *refs, width, rows, count):
    others = refs[: count - 1]
    noise_others = refs[count - 1 : 2 * (count - 1)]
    walk_end, short, flow = refs[-3:]
    value = moved[...]
    for other in others:
        value = value + other[...].astype(f32)
    flow[...] = value
    x = x_of()
    walk_end[...] = flow[:, pl.ds(pl.multiple_of(x * width, width), width)]
    t = times[rows, :]
    spread = jnp.sqrt(t * (1.0 - t)) * NOISE_LEVEL
    for shift in range(count):
        at = pl.ds(pl.multiple_of(lax.rem(x + shift, count) * width, width), width)
        noise = noise_mine if shift == 0 else noise_others[shift - 1]
        start = flow[:, at].astype(bf16).astype(f32)
        last = end[:, at].astype(f32)
        interpolant = (1.0 - t) * start + t * last + spread * noise[rows, :].astype(f32)
        short[:, at] = interpolant.astype(bf16)
        flow[:, at] = (last - interpolant) / (1.0 - t)


def fore_kernel(own, other, gain, expand, clock, reduce, times, *refs, width, rows, parts):
    other_out, own_out, active, slope, pieces, normed = refs
    norm_into(normed, own, other, gain, width)
    spread_out(normed, pieces, parts)
    t = times[rows, :]
    for start in range(0, expand.shape[1], TILE):
        cut = slice(start, start + TILE)
        hidden = dot(normed[...], expand[:, cut]) + t * clock[:, cut]
        sigmoid = 1.0 / (1.0 + jnp.exp(-hidden))
        active[:, cut] = (hidden * sigmoid).astype(bf16)
        slope[:, cut] = sigmoid * (1.0 + hidden * (1.0 - sigmoid))
    reduce_out(active, reduce, other_out, own_out, width)


def spread_out(whole, pieces, parts):
    count = whole.shape[0] // parts
    width = pieces.shape[2]
    start = pl.multiple_of(lax.axis_index("tensor") * count, count)
    share = whole[pl.ds(start, count), :]
    for to in range(pieces.shape[0]):
        pieces[to] = share[:, to * width : (to + 1) * width]


def sum_kernel(own, other, total, sent):
    value = own[...] + other[...].astype(f32)
    total[...] = value
    sent[...] = value.astype(bf16)


def error_kernel(total, flow, *refs, scale, count):
    *others, error = refs[: count - 1] + refs[-1:]
    value = total[...]
    for other in others:
        value = value + other[...].astype(f32)
    error[...] = ((value - flow[...]) * scale).astype(bf16)


def back_kernel(own, other, reduce, slope, hidden_grad, pieces, error, *, width, parts):
    core = core_of()
    for who, rows in ((core, own), (1 - core, other)):
        for x in range(rows.shape[1] // width):
            error[:, pl.ds(block_of(who, x, width), width)] = rows[:, x * width : (x + 1) * width]
    spread_out(error, pieces, parts)
    for start in range(0, reduce.shape[0], TILE):
        cut = slice(start, start + TILE)
        product = lax.dot_general(
            error[...], reduce[cut, :], (((1,), (1,)), ((), ())), preferred_element_type=f32
        )
        hidden_grad[:, cut] = (product * slope[:, cut]).astype(bf16)


def turn_kernel(*refs, chunks):
    *groups, out, gathered = refs
    me = lax.axis_index("tensor")
    batch, count, width = groups[0].shape
    share = count // chunks
    rows = share * len(groups)
    for shift in range(batch):
        source = before(shift, batch)
        for chunk in range(chunks):
            for step, group in enumerate(groups):
                member = jnp.bitwise_xor(me, step)
                gathered[member] = group[source, chunk * share : (chunk + 1) * share, :].astype(f32)
            whole = gathered[...].reshape(rows, width)
            start = (shift * chunks + chunk) * rows
            out[:, start : start + rows] = whole.T.astype(bf16)


def grad_kernel(left, *refs):
    *blocks, out = refs
    rows = blocks[0].shape[0]
    for start in range(0, out.shape[1], TILE):
        cut = slice(start, start + TILE)
        total = None
        for index in range(0, len(blocks), 2):
            pair = jnp.concatenate([blocks[index][:, cut], blocks[index + 1][:, cut]], axis=0)
            product = dot(left[:, index * rows : (index + 2) * rows], pair)
            total = product if total is None else total + product
        out[:, cut] = total


GATHER_MOST = 8


def make_body(batch, tensor):
    across = tensor // 2

    def swap_core(value):
        return lax.ppermute(value, "tensor", [(j, j ^ 1) for j in range(tensor)])

    def pass_x(value):
        return [
            lax.ppermute(
                value, "tensor", [(2 * ((x + s) % across) + c, 2 * x + c) for x in range(across) for c in (0, 1)]
            )
            for s in range(1, across)
        ]

    def turn(value, shift):
        ring = list(range(0, batch, 2)) + list(range(1, batch, 2))[::-1]
        pairs = [(ring[p], ring[(p + shift) % batch]) for p in range(batch)]
        return lax.ppermute(value, "batch", pairs)

    def exchange(value):
        return lax.all_to_all(value, "batch", split_axis=0, concat_axis=0, tiled=True)

    def ring_gather(values):
        found = [[None] * batch for _ in values]
        for chunk, value in enumerate(values):
            found[chunk][0] = value
        ahead = [batch // 2 - chunk % 2 for chunk in range(len(values))]
        for hop in range(1, batch // 2 + 1):
            for chunk in range(len(values)):
                if hop <= ahead[chunk]:
                    found[chunk][hop] = turn(found[chunk][hop - 1], 1)
                if hop <= batch - 1 - ahead[chunk]:
                    found[chunk][batch - hop] = turn(found[chunk][(batch - hop + 1) % batch], -1)
        return found

    def body(
        target_latents, walk_noise, step_sizes, back_gain, back_expand, back_clock, back_reduce,
        bridge_times, bridge_noise, fore_gain, fore_expand, fore_clock, fore_reduce,
    ):
        rows, width = target_latents.shape
        steps = walk_noise.shape[0]
        features, units = back_expand.shape
        half = features // 2
        count = rows // CHUNKS
        chunks = range(CHUNKS)
        cuts = [slice(chunk * count, (chunk + 1) * count) for chunk in chunks]
        gain_b, clock_b = back_gain[None, :], back_clock[None, :]
        gain_f, clock_f = fore_gain[None, :], fore_clock[None, :]

        state, own, ends = [], [], []
        for chunk in chunks:
            mine = target_latents[cuts[chunk]]
            joined, first = call(
                functools.partial(join_kernel, width=width),
                [shape((count, half), bf16), shape((count, half), f32)],
                [VMEM] * across,
                [mine, *pass_x(mine)],
            )
            own.append(joined)
            ends.append(joined)
            state.append(first)
        other = [swap_core(own[chunk]) for chunk in chunks]

        packed = call(
            pack_kernel,
            [shape((rows, width + 128), bf16)],
            [VMEM] * 2,
            [bridge_noise, bridge_times[:, None]],
        )[0]
        noise, times = call(
            unpack_kernel,
            [shape((rows, width), bf16), shape((rows, 1), f32)],
            [VMEM],
            [exchange(packed)],
        )
        noise_others = pass_x(noise)

        moved, passed, kept, sent = [None] * CHUNKS, [None] * CHUNKS, [None] * CHUNKS, [None] * CHUNKS

        def walk(step, chunk):
            away, kept = call(
                functools.partial(walk_kernel, width=width, step=step),
                [shape((count, half), bf16), shape((count, half), f32)],
                [SMEM] + [VMEM] * 6,
                [step_sizes, own[chunk], other[chunk], gain_b, back_expand, clock_b, back_reduce],
                [pltpu.VMEM((count, features), bf16), pltpu.VMEM((count, units), bf16)],
                flops=4 * count * features * units,
            )
            sent[chunk], moved[chunk] = call(
                functools.partial(move_kernel, width=width, step=step, rows=cuts[chunk]),
                [shape((count, half), bf16), shape((count, half), f32)],
                [SMEM] + [VMEM] * 4,
                [step_sizes, kept, swap_core(away), state[chunk], walk_noise],
            )
            passed[chunk] = pass_x(sent[chunk])

        def land(chunk):
            state[chunk], own[chunk] = call(
                functools.partial(land_kernel, count=across),
                [shape((count, half), f32), shape((count, half), bf16)],
                [VMEM] * across + [ANY],
                [moved[chunk], *passed[chunk], sent[chunk - 1]],
            )
            other[chunk] = swap_core(own[chunk])

        for chunk in chunks:
            walk(0, chunk)
        for step in range(1, steps):
            for chunk in chunks:
                land(chunk)
                walk(step, chunk)

        walk_end, flow = [None] * CHUNKS, [None] * CHUNKS
        active, slope, normed, pieces, total = ([None] * CHUNKS for _ in range(5))
        piece = shape((batch, count // tensor, features // batch), bf16)
        for chunk in chunks:
            walk_end[chunk], own[chunk], flow[chunk] = call(
                functools.partial(bridge_kernel, width=width, rows=cuts[chunk], count=across),
                [shape((count, width), f32), shape((count, half), bf16), shape((count, half), f32)],
                [VMEM] * (4 + 2 * (across - 1)) + [ANY],
                [moved[chunk], ends[chunk], times, noise, *passed[chunk], *noise_others, sent[chunk - 1]],
            )
            away, kept, active[chunk], slope[chunk], pieces[chunk], normed[chunk] = call(
                functools.partial(fore_kernel, width=width, rows=cuts[chunk], parts=tensor),
                [
                    shape((count, half), bf16),
                    shape((count, half), f32),
                    shape((count, units), bf16),
                    shape((count, units), f32),
                    piece,
                    shape((count, features), bf16),
                ],
                [VMEM] * 7,
                [own[chunk], swap_core(own[chunk]), gain_f, fore_expand, clock_f, fore_reduce, times],
                flops=4 * count * features * units,
            )
            total[chunk], sent[chunk] = call(
                sum_kernel,
                [shape((count, half), f32), shape((count, half), bf16)],
                [VMEM] * 2,
                [kept, swap_core(away)],
            )
            passed[chunk] = pass_x(sent[chunk])

        scale = float(rows * batch) ** -0.5
        hidden_grad, error, error_pieces = ([None] * CHUNKS for _ in range(3))
        for chunk in chunks:
            short = call(
                functools.partial(error_kernel, scale=scale, count=across),
                [shape((count, half), bf16)],
                [VMEM] * (1 + across) + [ANY],
                [total[chunk], flow[chunk], *passed[chunk], sent[chunk - 1]],
            )[0]
            hidden_grad[chunk], error_pieces[chunk], error[chunk] = call(
                functools.partial(back_kernel, width=width, parts=tensor),
                [shape((count, units), bf16), piece, shape((count, features), bf16)],
                [VMEM] * 4,
                [short, swap_core(short), fore_reduce, slope[chunk]],
                flops=2 * count * features * units,
            )

        def left_side(pieces):
            mine = exchange(jnp.concatenate(pieces, axis=1))
            far = pass_x(mine)[0]
            return call(
                functools.partial(turn_kernel, chunks=CHUNKS),
                [shape((features // batch, batch * rows), bf16)],
                [VMEM] * 4,
                [mine, swap_core(mine), far, swap_core(far)],
                [pltpu.VMEM((tensor, count // tensor, features // batch), f32)],
            )[0]

        def gradient(left, gathered):
            blocks = [gathered[chunk][shift] for shift in range(batch) for chunk in chunks]
            return call(
                grad_kernel,
                [shape((features // batch, units), f32)],
                [VMEM] * (1 + len(blocks)),
                [left, *blocks],
                flops=2 * rows * batch * units * features // batch,
            )[0]

        def summed(left, right):
            left, right = jnp.concatenate(left), jnp.concatenate(right)
            part = lax.dot_general(left, right, (((0,), (0,)), ((), ())), preferred_element_type=f32)
            return lax.psum_scatter(part, "batch", scatter_dimension=0, tiled=True)

        if batch > GATHER_MOST or tensor != 4:
            grad_expand, grad_reduce_t = summed(normed, hidden_grad), summed(error, active)
        else:
            all_active = ring_gather(active)
            left_normed = left_side(pieces)
            all_grads = ring_gather(hidden_grad)
            left_error = left_side(error_pieces)
            grad_reduce_t = gradient(left_error, all_active)
            grad_expand = gradient(left_normed, all_grads)
        return (jnp.concatenate(walk_end), grad_expand, grad_reduce_t)

    return body


def solution(mesh):
    placed = (
        P("batch", "tensor"),
        P(None, "batch", "tensor"),
        P(),
        P(),
        P(None, "tensor"),
        P("tensor"),
        P("tensor", None),
        P("batch"),
        P("batch", "tensor"),
        P(),
        P(None, "tensor"),
        P("tensor"),
        P("tensor", None),
    )
    return jax.shard_map(
        make_body(mesh.shape["batch"], mesh.shape["tensor"]),
        mesh=mesh,
        in_specs=placed,
        out_specs=(P("batch", "tensor"), P("batch", "tensor"), P("batch", "tensor")),
        check_vma=False,
    )
```
